32 devices in a mesh: groups: 2 (over y), space: 16 (over z, x, core).
Axes of the slice: x: 2, y: 2, z: 4, core: 2. Of those that a mesh axis runs over, the one named last changes fastest.
Arguments:
- wavefield: bfloat16 [8192, 1024], P(('groups', 'space')), parts along dimension 0, may hold values from -6 to 6
- redatum_taps: float32 [512, 65], P('groups'), parts along dimension 0, may hold values from -0.75 to 0.75
- cell_x: int32 [5, 16384], replicated, may hold values from 0 to 4095
- cell_depth: int32 [16384], replicated, may hold values from 1 to 511
- slowness: float32 [4], replicated, may hold values from 0.02 to 0.2
- illumination: float32 [32768], P('groups'), parts along dimension 0, may hold values from 0.3 to 3
- aperture: int32 [8192, 1024], P(('groups', 'space')), parts along dimension 0, may hold values 0 or 1
Outputs:
- image: float32 [32, 1024], P(('groups', 'space')), parts along dimension 0
The draws below stay inside these ranges and needn't reach their ends.
There are 2 independent parts, one for each index of `groups`. The reference program is written for one: setup_inputs(seed, part) draws one part's arguments, and reference() takes and returns one part's arrays. A program takes and returns all parts, laid end to end along the dimension named above; an argument that names none is the same for every part. Nothing has to cross between parts.
All inputs are finite; a program needn't handle non-finite values. No bound on the sum of `aperture` on one device may be relied on, other than what follows from the above.
Results may differ from the reference program's by a relative error of at most 0.0075.
Values may be sent and summed in bfloat16 or wider, within the bound.
A program may use at most 64 MiB of HBM per device.

```python
import math
import jax
import jax.numpy as jnp
from jax import lax

M = 1024
NF = 256
H = 32
LEVELS = 4
TAPS = 65
BOXES = 16
FREQS = 256
N_SPACE = 16


def touch_ends(array, rng, least, largest):
    longest = array.shape.index(max(array.shape))
    spots = []
    for shift in (0, 1):
        where = [jax.random.randint(jax.random.fold_in(rng, axis), (), 0, length) for axis, length in enumerate(array.shape)]
        where[longest] = (where[longest] + shift) % array.shape[longest]
        spots.append(tuple(where))
    return array.at[spots[0]].set(least).at[spots[1]].set(largest)


def level_of(key, shape, cuts, least, high):
    loudness, own = 1.0, jax.random.fold_in(key, 6)
    for position, parts in cuts:
        steps = jnp.exp(jax.random.uniform(jax.random.fold_in(own, position), (parts,), jnp.float32, least / len(cuts), high / len(cuts)))
        loudness = loudness * jnp.repeat(steps, shape[position] // parts).reshape([-1 if axis == position else 1 for axis in range(len(shape))])
    return loudness


def normal_values(key, extent, spread, limit, pieces=(), held_as=jnp.bfloat16):
    array = jax.random.normal(key, extent, jnp.float32) * spread
    if len(pieces) > 0:
        array = level_of(key, extent, pieces, -0.22, 0.18) * array
    return jnp.clip(array, min=-limit, max=limit).astype(held_as)


def setup_inputs(seed: int = 0, part: int = 0) -> dict:
    arg_keys = jax.random.split(jax.random.key(seed), 8)
    part_keys = jax.random.split(jax.random.fold_in(arg_keys[7], part), 8)
    return {
        "wavefield": normal_values(part_keys[0], (N_SPACE * NF, M), 1.0, 6.0, ((0, 16),)),
        "redatum_taps": normal_values(part_keys[1], (FREQS, TAPS), TAPS ** -0.5, 0.75, (), jnp.float32),
        "cell_x": touch_ends(jax.random.randint(arg_keys[2], (LEVELS + 1, BOXES * M), 0, 4096), jax.random.fold_in(arg_keys[2], 1), 0, 4095).astype(jnp.int32),
        "cell_depth": touch_ends(jax.random.randint(arg_keys[3], (BOXES * M,), 1, 512), jax.random.fold_in(arg_keys[3], 1), 1, 511).astype(jnp.int32),
        "slowness": jnp.clip(jnp.exp(jax.random.uniform(arg_keys[4], (LEVELS,), jnp.float32, math.log(0.02), math.log(0.2))), 0.02, 0.2),
        "illumination": jnp.clip(jnp.exp(jax.random.uniform(part_keys[5], (BOXES * M,), jnp.float32, math.log(0.3), math.log(3.0))), 0.3, 3.0),
        "aperture": touch_ends((jax.random.randint(part_keys[6], (N_SPACE * NF, M), 0, 3) < 2).astype(jnp.int32), jax.random.fold_in(part_keys[6], 1), 0, 1),
    }


def translator(rows_x, cols_x, cols_depth, slow, width):
    across = (rows_x[:, None] - cols_x[None, :]).astype(jnp.float32)
    depth = cols_depth.astype(jnp.float32)[None, :]
    travel = jnp.sqrt(across * across + depth * depth)
    return (jnp.cos(slow * travel) / jnp.sqrt(jnp.float32(width))).astype(jnp.bfloat16)

def redatum(padded, taps, width):
    total = taps[..., 0:1] * padded[..., 0:width]
    for shift in range(1, taps.shape[-1]):
        total = total + taps[..., shift:shift + 1] * padded[..., shift:shift + width]
    return total

def reference(wavefield, redatum_taps, cell_x, cell_depth, slowness, illumination, aperture):
    blocks = N_SPACE // BOXES
    wave = wavefield.reshape(BOXES, blocks, NF, M).astype(jnp.float32)
    line = jnp.transpose(wave, (1, 2, 0, 3)).reshape(blocks, NF, BOXES * M)
    padded = jnp.pad(line, ((0, 0), (0, 0), (H, H)))
    taps = redatum_taps.reshape(blocks, NF, 2 * H + 1)
    moved = redatum(padded, taps, BOXES * M).astype(jnp.bfloat16)
    state = jnp.transpose(moved.reshape(blocks, NF, BOXES, M), (2, 0, 1, 3)).reshape(BOXES, blocks * NF, M)
    for level in range(LEVELS):
        bit = 1 << level
        outputs = []
        for box in range(BOXES):
            low = box - (box & bit)
            high = low + bit
            stacked = jnp.concatenate([state[low], state[high]], 1)
            rows_x = jnp.concatenate([cell_x[level, low * M:(low + 1) * M], cell_x[level, high * M:(high + 1) * M]])
            table = translator(rows_x, cell_x[level + 1, box * M:(box + 1) * M], cell_depth[box * M:(box + 1) * M], slowness[level], M)
            outputs.append(jnp.dot(stacked, table, preferred_element_type=jnp.float32))
        mixed = jnp.stack(outputs)
        state = mixed.astype(jnp.bfloat16) if level + 1 < LEVELS else mixed
    final = state.reshape(BOXES, blocks, NF, M)
    mask = aperture.reshape(BOXES, blocks, NF, M)
    partial_value = lax.optimization_barrier(jnp.sum(jnp.where(mask > 0, final, jnp.zeros_like(final)), 2))
    partial_value = partial_value * illumination.reshape(BOXES, 1, M) / jnp.sqrt(jnp.float32(NF * blocks))
    image = lax.optimization_barrier(jnp.sum(partial_value, 1))
    share = M // blocks
    return image.reshape(BOXES * blocks, share)
```

```python
import math

import jax
import jax.numpy as jnp
from jax import lax
from jax.sharding import PartitionSpec as P

LEVELS = 4
BOXES = 16


column_block = 256


def passed_along(shard, axis, by):
    devices = lax.axis_size(axis)
    pairs = [(i, i + by) for i in range(devices) if 0 <= i + by < devices]
    return lax.ppermute(shard, axis, pairs)


def partner(shard, axis, bit):
    return lax.ppermute(shard, axis, [(i, i ^ 1 << bit) for i in range(lax.axis_size(axis))])


SINE = (3.141574351665506, -5.166959589539674, 2.5406483216241926, -0.5520516912044007)


def cosine_of_turns(turns, scale):
    rest = turns - jnp.round(turns)
    square = rest * rest
    root = (2.0 * scale) ** 0.5
    half = jnp.float32(SINE[-1] * root)
    for value in SINE[-2::-1]:
        half = half * square + jnp.float32(value * root)
    return jnp.float32(scale) - square * (half * half)


def translator(rows_x, cols_x, cols_depth, slow, width):
    turn = slow * jnp.float32(0.5 / math.pi)
    across = (rows_x[:, None] - cols_x[None, :]).astype(jnp.float32) * turn
    depth = cols_depth.astype(jnp.float32)[None, :] * turn
    sums = across * across + depth * depth
    return cosine_of_turns(sums * lax.rsqrt(sums), width ** -0.5).astype(jnp.bfloat16)


def redatum(padded, taps, width):
    total = taps[..., 0:1] * padded[..., 0:width]
    for shift in range(1, taps.shape[-1]):
        total = total + taps[..., shift : shift + 1] * padded[..., shift : shift + width]
    return total


def translate(left, rows_x, cols_x, cols_depth, slow, width):
    step = min(column_block, cols_x.shape[0])
    pieces = []
    for start in range(0, cols_x.shape[0], step):
        table = translator(
            rows_x, cols_x[start : start + step], cols_depth[start : start + step], slow, width
        )
        pieces.append(jnp.dot(left, table, preferred_element_type=jnp.float32))
    return jnp.concatenate(pieces, 1)


def on_device(wavefield, redatum_taps, cell_x, cell_depth, slowness, illumination, aperture):
    index = lax.axis_index("space")
    devices = lax.axis_size("space")
    blocks = devices // BOXES
    block_bits = blocks.bit_length() - 1
    box = index // blocks
    block = index % blocks
    count = wavefield.shape[0]
    width = wavefield.shape[1]
    reach = (redatum_taps.shape[1] - 1) // 2
    below = passed_along(wavefield[:, width - reach :], "space", blocks)
    above = passed_along(wavefield[:, :reach], "space", -blocks)
    padded = jnp.concatenate([below, wavefield, above], 1).astype(jnp.float32)
    taps = lax.dynamic_slice_in_dim(redatum_taps, block * count, count, 0)
    state = redatum(padded, taps, width).astype(jnp.bfloat16)
    visiting = partner((aperture > 0).astype(jnp.bfloat16), "space", LEVELS - 1 + block_bits)
    for level in range(LEVELS):
        bit = 1 << level
        upper = box // bit % 2 == 1
        paired = box + jnp.where(upper, -bit, bit)
        own_rows = lax.dynamic_slice_in_dim(cell_x[level], box * width, width)
        far_rows = lax.dynamic_slice_in_dim(cell_x[level], paired * width, width)
        cols_x = lax.dynamic_slice_in_dim(cell_x[level + 1], box * width, width)
        cols_depth = lax.dynamic_slice_in_dim(cell_depth, box * width, width)
        slow = slowness[level]
        if level + 1 < LEVELS:
            far = partner(state, "space", level + block_bits)
            own_term = translate(state, own_rows, cols_x, cols_depth, slow, width)
            far_term = translate(far, far_rows, cols_x, cols_depth, slow, width)
            state = (own_term + far_term).astype(jnp.bfloat16)
        else:
            far_x = lax.dynamic_slice_in_dim(cell_x[level + 1], paired * width, width)
            far_depth = lax.dynamic_slice_in_dim(cell_depth, paired * width, width)
            far_term = translate(state, own_rows, far_x, far_depth, slow, width)
            far_sum = jnp.sum(far_term * visiting.astype(jnp.float32), 0)
            own_term = translate(state, own_rows, cols_x, cols_depth, slow, width)
            arrived = partner(far_sum, "space", level + block_bits)
            summed = jnp.sum(jnp.where(aperture > 0, own_term, jnp.zeros_like(own_term)), 0) + arrived
    weights = lax.dynamic_slice_in_dim(illumination, box * width, width)
    partial_image = summed * weights / jnp.sqrt(jnp.float32(count * blocks))
    for level in range(block_bits):
        partial_image = partial_image + partner(partial_image, "space", level)
    share = width // blocks
    image = lax.dynamic_slice_in_dim(partial_image, block * share, share)
    return image[None, :]


def solution(mesh):
    placed = (
        P(("groups", "space"), None),
        P("groups", None),
        P(),
        P(),
        P(),
        P("groups"),
        P(("groups", "space"), None),
    )
    return jax.shard_map(
        on_device,
        mesh=mesh,
        in_specs=placed,
        out_specs=P(("groups", "space"), None),
        check_vma=False,
    )
```

```python
import functools
import math

import jax
import jax.numpy as jnp
from jax import lax
from jax.experimental import pallas as pl
from jax.experimental.pallas import tpu as pltpu
from jax.sharding import PartitionSpec as P

LEVELS = 4
BOXES = 16
LANES = 128
COLUMNS = 256
TILE = 64
SINE = (3.141574351665506, -5.166959589539674, 2.5406483216241926, -0.5520516912044007)


def partner(shard, axis, bit):
    return lax.ppermute(shard, axis, [(i, i ^ 1 << bit) for i in range(lax.axis_size(axis))])


def cosine_of_turns(turns, scale):
    rest = turns - jnp.round(turns)
    square = rest * rest
    root = (2.0 * scale) ** 0.5
    half = jnp.float32(SINE[-1] * root)
    for value in SINE[-2::-1]:
        half = half * square + jnp.float32(value * root)
    return jnp.float32(scale) - square * (half * half)


def kernel(
    devices,
    wave_ref,
    taps_ref,
    cell_ref,
    depth_ref,
    slow_ref,
    light_ref,
    aperture_ref,
    out_ref,
    before_ref,
    after_ref,
    mask_ref,
    visiting_ref,
    line_ref,
    filter_ref,
    moved_ref,
    state_ref,
    far_ref,
    table_ref,
    sum_ref,
    arrived_ref,
    send_sem,
    recv_sem,
):
    index = lax.axis_index("space")
    blocks = devices // BOXES
    block_bits = blocks.bit_length() - 1
    box = index // blocks
    block = index % blocks
    count, width = wave_ref.shape
    taps = taps_ref.shape[1]
    reach = (taps - 1) // 2
    halves = count // LANES

    def flipped(value, bit):
        return value + bit - 2 * bit * (value // bit % 2)

    following = (index + blocks) % devices
    previous = (index + devices - blocks) % devices
    mates = [flipped(index, blocks << level) for level in range(LEVELS)]
    paired = [flipped(box, 1 << level) for level in range(LEVELS)]

    def copy(slot, source, target, device):
        return pltpu.make_async_remote_copy(
            src_ref=source,
            dst_ref=target,
            send_sem=send_sem.at[slot],
            recv_sem=recv_sem.at[slot],
            device_id={"space": device},
            device_id_type=pl.DeviceIdType.MESH,
        )

    barrier = pltpu.get_barrier_semaphore()
    for device in [following, previous] + mates:
        pl.semaphore_signal(
            barrier, inc=1, device_id={"space": device}, device_id_type=pl.DeviceIdType.MESH
        )
    pl.semaphore_wait(barrier, LEVELS + 2)

    copies = [
        copy(0, wave_ref.at[:, pl.ds(width - LANES, LANES)], before_ref, following),
        copy(1, wave_ref.at[:, pl.ds(0, LANES)], after_ref, previous),
    ]
    for halo in copies:
        halo.start()

    mask_ref[...] = (aperture_ref[...] > 0).astype(jnp.float32).astype(jnp.bfloat16)
    visit = copy(2, mask_ref, visiting_ref, mates[LEVELS - 1])
    visit.start()
    copies.append(visit)

    for half in range(halves):
        rows = pl.ds(half * LANES, LANES)
        filter_ref[half, :, pl.ds(0, taps)] = taps_ref[
            pl.ds(pl.multiple_of(block * count + half * LANES, LANES), LANES), :
        ]
        filter_ref[half] = filter_ref[half].T
        for part in range(width // LANES):
            piece = wave_ref[rows, pl.ds(part * LANES, LANES)].astype(jnp.float32)
            line_ref[half, pl.ds(reach + part * LANES, LANES), :] = piece.T

    def redatum(half, tile):
        start = pl.multiple_of(tile * TILE, TILE)
        total = jnp.zeros((TILE, LANES), jnp.float32)
        for shift in range(taps):
            total = total + filter_ref[half, pl.ds(shift, 1), :] * line_ref[half, pl.ds(start + shift, TILE), :]
        moved_ref[half, pl.ds(start, TILE), :] = total

    tiles = width // TILE
    edge = (reach + TILE - 1) // TILE

    for half in range(halves):
        pl.loop(edge, tiles - edge)(lambda tile, half=half: redatum(half, tile))
    copies[0].wait_recv()
    copies[1].wait_recv()
    for half in range(halves):
        rows = pl.ds(half * LANES, LANES)
        low = before_ref[rows, :].astype(jnp.float32).T[LANES - reach :, :]
        line_ref[half, pl.ds(0, reach), :] = jnp.where(box > 0, low, jnp.zeros_like(low))
        high = after_ref[rows, :].astype(jnp.float32).T[:reach, :]
        line_ref[half, pl.ds(reach + width, reach), :] = jnp.where(
            box < BOXES - 1, high, jnp.zeros_like(high)
        )
        pl.loop(0, edge)(lambda tile, half=half: redatum(half, tile))
        pl.loop(tiles - edge, tiles)(lambda tile, half=half: redatum(half, tile))
        for part in range(width // LANES):
            columns = pl.ds(part * LANES, LANES)
            state_ref[0, rows, columns] = moved_ref[half, columns, :].T.astype(jnp.bfloat16)

    def fill(slot, level, rows_box, cols_box):
        turn = slow_ref[level] * jnp.float32(0.5 / math.pi)
        across, deep = [], []
        for part in range(width // LANES):
            start = pl.multiple_of(cols_box * width + part * LANES, LANES)
            across.append(cell_ref[pl.ds(level + 1, 1), pl.ds(start, LANES)].astype(jnp.float32) * turn)
            depth = depth_ref[pl.ds(cols_box * (width // LANES) + part, 1), :].astype(jnp.float32) * turn
            deep.append(depth * depth)

        @pl.loop(0, width // LANES)
        def _(group):
            start = pl.multiple_of(rows_box * width + group * LANES, LANES)
            rows = cell_ref[pl.ds(level, 1), pl.ds(start, LANES)].astype(jnp.float32) * turn
            tall = jnp.broadcast_to(rows, (LANES, LANES)).T
            for piece in range(LANES // 16):
                own = tall[piece * 16 : piece * 16 + 16]
                for part in range(width // LANES):
                    apart = own - across[part]
                    sums = apart * apart + deep[part]
                    table = cosine_of_turns(sums * lax.rsqrt(sums), width ** -0.5)
                    table_ref[
                        slot,
                        pl.ds(pl.multiple_of(group * LANES + piece * 16, 16), 16),
                        pl.ds(part * LANES, LANES),
                    ] = table.astype(jnp.bfloat16)

    def term(left, slot, columns):
        return jnp.dot(left, table_ref[slot, :, columns], preferred_element_type=jnp.float32)

    def send(level):
        moving = copy(3 + level, state_ref.at[level], far_ref.at[level], mates[level])
        moving.start()
        copies.append(moving)
        return moving

    last = LEVELS - 1
    plan = [(2 * level + side, level, (box, paired[level])[side], box) for level in range(last) for side in (0, 1)]
    plan += [(2 * last, last, box, paired[last]), (2 * last + 1, last, box, box)]
    ahead = (2, 5, len(plan))
    done = 0
    for level in range(last):
        moving = send(level)
        while done < ahead[level]:
            fill(*plan[done])
            done += 1
        moving.wait_recv()

        @pl.loop(0, width // COLUMNS)
        def _(part):
            columns = pl.ds(pl.multiple_of(part * COLUMNS, COLUMNS), COLUMNS)
            mixed = term(state_ref[level], 2 * level, columns) + term(far_ref[level], 2 * level + 1, columns)
            state_ref[level + 1, :, columns] = mixed.astype(jnp.bfloat16)

    visit.wait_recv()

    @pl.loop(0, width // COLUMNS)
    def _(part):
        columns = pl.ds(pl.multiple_of(part * COLUMNS, COLUMNS), COLUMNS)
        mixed = term(state_ref[last], 2 * last, columns)
        kept = jnp.where(visiting_ref[:, columns].astype(jnp.float32) > 0, mixed, jnp.zeros_like(mixed))
        sum_ref[:, columns] = jnp.sum(kept, 0, keepdims=True)

    final = copy(3 + last, sum_ref, arrived_ref, mates[last])
    final.start()
    copies.append(final)

    @pl.loop(0, width // COLUMNS)
    def _(part):
        columns = pl.ds(pl.multiple_of(part * COLUMNS, COLUMNS), COLUMNS)
        mixed = term(state_ref[last], 2 * last + 1, columns)
        kept = jnp.where(aperture_ref[:, columns] > 0, mixed, jnp.zeros_like(mixed))
        out_ref[:, columns] = jnp.sum(kept, 0, keepdims=True)

    final.wait_recv()
    for part in range(width // LANES):
        columns = pl.ds(part * LANES, LANES)
        weights = light_ref[pl.ds(box * (width // LANES) + part, 1), :]
        both = out_ref[:, columns] + arrived_ref[:, columns]
        out_ref[:, columns] = both * weights * jnp.float32((count * blocks) ** -0.5)
    for moving in copies:
        moving.wait_send()


def on_device(wavefield, redatum_taps, cell_x, cell_depth, slowness, illumination, aperture):
    index = lax.axis_index("space")
    devices = lax.axis_size("space")
    blocks = devices // BOXES
    block_bits = blocks.bit_length() - 1
    count, width = wavefield.shape
    reach = (redatum_taps.shape[1] - 1) // 2
    halves = count // LANES
    vmem = pl.BlockSpec(memory_space=pltpu.VMEM)
    smem = pl.BlockSpec(memory_space=pltpu.SMEM)
    partial_image = pl.pallas_call(
        functools.partial(kernel, devices),
        out_shape=jax.ShapeDtypeStruct((1, width), jnp.float32),
        in_specs=[vmem, vmem, vmem, vmem, smem, vmem, vmem],
        out_specs=vmem,
        scratch_shapes=[
            pltpu.VMEM((count, LANES), jnp.bfloat16),
            pltpu.VMEM((count, LANES), jnp.bfloat16),
            pltpu.VMEM((count, width), jnp.bfloat16),
            pltpu.VMEM((count, width), jnp.bfloat16),
            pltpu.VMEM((halves, width + 2 * reach, LANES), jnp.float32),
            pltpu.VMEM((halves, LANES, LANES), jnp.float32),
            pltpu.VMEM((halves, width, LANES), jnp.float32),
            pltpu.VMEM((LEVELS, count, width), jnp.bfloat16),
            pltpu.VMEM((LEVELS - 1, count, width), jnp.bfloat16),
            pltpu.VMEM((2 * LEVELS, width, width), jnp.bfloat16),
            pltpu.VMEM((1, width), jnp.float32),
            pltpu.VMEM((1, width), jnp.float32),
            pltpu.SemaphoreType.DMA((LEVELS + 3,)),
            pltpu.SemaphoreType.DMA((LEVELS + 3,)),
        ],
        compiler_params=pltpu.CompilerParams(
            collective_id=0, has_side_effects=True, vmem_limit_bytes=60 * 1024 * 1024
        ),
        name="migrate",
    )(
        wavefield,
        redatum_taps,
        cell_x,
        cell_depth.reshape(-1, LANES),
        slowness,
        illumination.reshape(-1, LANES),
        aperture,
    )
    for level in range(block_bits):
        partial_image = partial_image + partner(partial_image, "space", level)
    share = width // blocks
    return lax.dynamic_slice_in_dim(partial_image, index % blocks * share, share, 1)


def solution(mesh):
    placed = (
        P(("groups", "space"), None),
        P("groups", None),
        P(),
        P(),
        P(),
        P("groups"),
        P(("groups", "space"), None),
    )
    return jax.shard_map(
        on_device,
        mesh=mesh,
        in_specs=placed,
        out_specs=P(("groups", "space"), None),
        check_vma=False,
    )
```

```python
import functools
import math

import jax
import jax.numpy as jnp
from jax import lax
from jax.experimental import pallas as pl
from jax.experimental.pallas import tpu as pltpu
from jax.sharding import PartitionSpec as P

LEVELS = 4
BOXES = 16
LANES = 128
COLUMNS = 256
TILE = 64
HALF_COSINE = (0.9999982888639185, -4.934458868248177, 4.048770768883701, -1.2477951603331165)


def partner(shard, axis, bit):
    return lax.ppermute(shard, axis, [(i, i ^ 1 << bit) for i in range(lax.axis_size(axis))])


def cosine_of_turns(turns, scale):
    rest = turns - jnp.round(turns)
    square = rest * rest
    root = (2.0 * scale) ** 0.5
    half = jnp.float32(HALF_COSINE[-1] * root)
    for value in HALF_COSINE[-2::-1]:
        half = half * square + jnp.float32(value * root)
    return half * half - jnp.float32(scale)


def kernel(
    devices,
    wave_ref,
    taps_ref,
    cell_ref,
    depth_ref,
    slow_ref,
    light_ref,
    aperture_ref,
    out_ref,
    before_ref,
    after_ref,
    mask_ref,
    visiting_ref,
    line_ref,
    own_ref,
    last_ref,
    sum_ref,
    arrived_ref,
    send_sem,
    recv_sem,
    *large_refs,
):
    tables = large_refs[: 2 * LEVELS]
    states = large_refs[2 * LEVELS : 3 * LEVELS - 1]
    fars = large_refs[3 * LEVELS - 1 :]
    index = lax.axis_index("space")
    blocks = devices // BOXES
    box = index // blocks
    block = index % blocks
    count, width = wave_ref.shape
    taps = taps_ref.shape[0]
    reach = (taps - 1) // 2
    halves = count // LANES

    def flipped(value, bit):
        return value + bit - 2 * bit * (value // bit % 2)

    following = (index + blocks) % devices
    previous = (index + devices - blocks) % devices
    mates = [flipped(index, blocks << level) for level in range(LEVELS)]
    paired = [flipped(box, 1 << level) for level in range(LEVELS)]

    def copy(slot, source, target, device):
        return pltpu.make_async_remote_copy(
            src_ref=source,
            dst_ref=target,
            send_sem=send_sem.at[slot],
            recv_sem=recv_sem.at[slot],
            device_id={"space": device},
            device_id_type=pl.DeviceIdType.MESH,
        )

    barrier = pltpu.get_barrier_semaphore()
    for device in [following, previous] + mates:
        pl.semaphore_signal(
            barrier, inc=1, device_id={"space": device}, device_id_type=pl.DeviceIdType.MESH
        )
    pl.semaphore_wait(barrier, LEVELS + 2)

    copies = [
        copy(0, wave_ref.at[:, pl.ds(width - LANES, LANES)], before_ref, following),
        copy(1, wave_ref.at[:, pl.ds(0, LANES)], after_ref, previous),
    ]
    for halo in copies:
        halo.start()

    mask_ref[...] = (aperture_ref[...] > 0).astype(jnp.float32).astype(jnp.bfloat16)
    visit = copy(2, mask_ref, visiting_ref, mates[LEVELS - 1])
    visit.start()
    copies.append(visit)

    for half in range(halves):
        rows = pl.ds(half * LANES, LANES)
        for part in range(width // LANES):
            piece = wave_ref[rows, pl.ds(part * LANES, LANES)].astype(jnp.float32)
            line_ref[half, pl.ds(reach + part * LANES, LANES), :] = piece.T

    def redatum(half, tile):
        start = pl.multiple_of(tile * TILE, TILE)
        columns = pl.ds(pl.multiple_of(block * count + half * LANES, LANES), LANES)
        total = jnp.zeros((TILE, LANES), jnp.float32)
        for shift in range(taps):
            total = total + taps_ref[pl.ds(shift, 1), columns] * line_ref[half, pl.ds(start + shift, TILE), :]
        states[0][pl.ds(start, TILE), pl.ds(half * LANES, LANES)] = total.astype(jnp.bfloat16)

    tiles = width // TILE
    edge = (reach + TILE - 1) // TILE

    for half in range(halves):
        pl.loop(edge, tiles - edge)(lambda tile, half=half: redatum(half, tile))
    copies[0].wait_recv()
    copies[1].wait_recv()
    for half in range(halves):
        rows = pl.ds(half * LANES, LANES)
        low = before_ref[rows, :].astype(jnp.float32).T[LANES - reach :, :]
        line_ref[half, pl.ds(0, reach), :] = jnp.where(box > 0, low, jnp.zeros_like(low))
        high = after_ref[rows, :].astype(jnp.float32).T[:reach, :]
        line_ref[half, pl.ds(reach + width, reach), :] = jnp.where(
            box < BOXES - 1, high, jnp.zeros_like(high)
        )
        pl.loop(0, edge)(lambda tile, half=half: redatum(half, tile))
        pl.loop(tiles - edge, tiles)(lambda tile, half=half: redatum(half, tile))

    def fill(table, tall, flat, deep_is_tall, beside=None):
        turn = slow_ref[min(tall[0], flat[0])] * jnp.float32(0.5 / math.pi)
        across, deep = [], []
        for part in range(width // LANES):
            start = pl.multiple_of(flat[1] * width + part * LANES, LANES)
            across.append(cell_ref[pl.ds(flat[0], 1), pl.ds(start, LANES)].astype(jnp.float32) * turn)
            if not deep_is_tall:
                depth = depth_ref[pl.ds(flat[1] * (width // LANES) + part, 1), :].astype(jnp.float32) * turn
                deep.append(depth * depth)

        @pl.loop(0, width // LANES)
        def _(group):
            start = pl.multiple_of(tall[1] * width + group * LANES, LANES)
            rows = cell_ref[pl.ds(tall[0], 1), pl.ds(start, LANES)].astype(jnp.float32) * turn
            high = jnp.broadcast_to(rows, (LANES, LANES)).T
            if deep_is_tall:
                depth = depth_ref[pl.ds(tall[1] * (width // LANES) + group, 1), :].astype(jnp.float32) * turn
                sunk = jnp.broadcast_to(depth * depth, (LANES, LANES)).T
            for piece in range(LANES // 16):
                own = high[piece * 16 : piece * 16 + 16]
                for pair in range(width // (2 * LANES)):
                    both = []
                    for part in (2 * pair, 2 * pair + 1):
                        apart = own - across[part]
                        below = sunk[piece * 16 : piece * 16 + 16] if deep_is_tall else deep[part]
                        sums = apart * apart + below
                        both.append(cosine_of_turns(sums * lax.rsqrt(sums), width ** -0.5))
                    table[
                        pl.ds(pl.multiple_of(group * LANES + piece * 16, 16), 16),
                        pl.ds(pair * 2 * LANES, 2 * LANES),
                    ] = jnp.concatenate(both, 1).astype(jnp.bfloat16)
            if beside is not None:
                beside(pl.ds(pl.multiple_of(group * LANES, LANES), LANES))

    def product(table, rows, right):
        return jnp.dot(table[rows, :], right[...], preferred_element_type=jnp.float32)

    def own_term(level):
        def beside(rows):
            own_ref[rows, :] = product(tables[2 * level], rows, states[level])

        return beside

    last = LEVELS - 1
    plan = []
    for level in range(last):
        for side in (box, paired[level]):
            plan.append((tables[len(plan)], (level + 1, box), (level, side), True))
    plan.append((tables[2 * last], (last, box), (last + 1, paired[last]), False))
    plan.append((tables[2 * last + 1], (last, box), (last + 1, box), False))
    order = ((0, 1), (2, 3, 4), (5, 6, 7))
    for level in range(last):
        moving = copy(3 + level, states[level], fars[level], mates[level])
        moving.start()
        copies.append(moving)
        for number in order[level]:
            fill(*plan[number], own_term(level) if number == 2 * level + (1 if level < last - 1 else 2) else None)
        moving.wait_recv()

        @pl.loop(0, width // COLUMNS)
        def _(part, level=level):
            rows = pl.ds(pl.multiple_of(part * COLUMNS, COLUMNS), COLUMNS)
            mixed = own_ref[rows, :] + product(tables[2 * level + 1], rows, fars[level])
            if level + 1 < last:
                states[level + 1][rows, :] = mixed.astype(jnp.bfloat16)
            else:
                last_ref[:, rows] = mixed.T.astype(jnp.bfloat16)

    visit.wait_recv()

    @pl.loop(0, width // COLUMNS)
    def _(part):
        columns = pl.ds(pl.multiple_of(part * COLUMNS, COLUMNS), COLUMNS)
        mixed = jnp.dot(last_ref[...], tables[2 * last][:, columns], preferred_element_type=jnp.float32)
        kept = jnp.where(visiting_ref[:, columns].astype(jnp.float32) > 0, mixed, jnp.zeros_like(mixed))
        sum_ref[:, columns] = jnp.sum(kept, 0, keepdims=True)

    final = copy(3 + last, sum_ref, arrived_ref, mates[last])
    final.start()
    copies.append(final)

    @pl.loop(0, width // COLUMNS)
    def _(part):
        columns = pl.ds(pl.multiple_of(part * COLUMNS, COLUMNS), COLUMNS)
        mixed = jnp.dot(last_ref[...], tables[2 * last + 1][:, columns], preferred_element_type=jnp.float32)
        kept = jnp.where(aperture_ref[:, columns] > 0, mixed, jnp.zeros_like(mixed))
        out_ref[:, columns] = jnp.sum(kept, 0, keepdims=True)

    final.wait_recv()
    for part in range(width // LANES):
        columns = pl.ds(part * LANES, LANES)
        weights = light_ref[pl.ds(box * (width // LANES) + part, 1), :]
        both = out_ref[:, columns] + arrived_ref[:, columns]
        out_ref[:, columns] = both * weights * jnp.float32((count * blocks) ** -0.5)
    for moving in copies:
        moving.wait_send()


def on_device(wavefield, redatum_taps, cell_x, cell_depth, slowness, illumination, aperture):
    index = lax.axis_index("space")
    devices = lax.axis_size("space")
    blocks = devices // BOXES
    block_bits = blocks.bit_length() - 1
    count, width = wavefield.shape
    reach = (redatum_taps.shape[1] - 1) // 2
    halves = count // LANES
    vmem = pl.BlockSpec(memory_space=pltpu.VMEM)
    smem = pl.BlockSpec(memory_space=pltpu.SMEM)
    partial_image = pl.pallas_call(
        functools.partial(kernel, devices),
        out_shape=jax.ShapeDtypeStruct((1, width), jnp.float32),
        in_specs=[vmem, vmem, vmem, vmem, smem, vmem, vmem],
        out_specs=vmem,
        scratch_shapes=[
            pltpu.VMEM((count, LANES), jnp.bfloat16),
            pltpu.VMEM((count, LANES), jnp.bfloat16),
            pltpu.VMEM((count, width), jnp.bfloat16),
            pltpu.VMEM((count, width), jnp.bfloat16),
            pltpu.VMEM((halves, width + 2 * reach, LANES), jnp.float32),
            pltpu.VMEM((width, count), jnp.float32),
            pltpu.VMEM((count, width), jnp.bfloat16),
            pltpu.VMEM((1, width), jnp.float32),
            pltpu.VMEM((1, width), jnp.float32),
            pltpu.SemaphoreType.DMA((LEVELS + 3,)),
            pltpu.SemaphoreType.DMA((LEVELS + 3,)),
        ]
        + [pltpu.VMEM((width, width), jnp.bfloat16)] * (2 * LEVELS)
        + [pltpu.VMEM((width, count), jnp.bfloat16)] * (2 * LEVELS - 2),
        compiler_params=pltpu.CompilerParams(
            collective_id=0, has_side_effects=True, vmem_limit_bytes=60 * 1024 * 1024
        ),
        name="migrate",
    )(
        wavefield,
        redatum_taps.T,
        cell_x,
        cell_depth.reshape(-1, LANES),
        slowness,
        illumination.reshape(-1, LANES),
        aperture,
    )
    for level in range(block_bits):
        partial_image = partial_image + partner(partial_image, "space", level)
    share = width // blocks
    return lax.dynamic_slice_in_dim(partial_image, index % blocks * share, share, 1)


def solution(mesh):
    placed = (
        P(("groups", "space"), None),
        P("groups", None),
        P(),
        P(),
        P(),
        P("groups"),
        P(("groups", "space"), None),
    )
    return jax.shard_map(
        on_device,
        mesh=mesh,
        in_specs=placed,
        out_specs=P(("groups", "space"), None),
        check_vma=False,
    )
```
